32 devices in a mesh: expert: 8 (over y, x, core), tensor: 4 (over z).
Axes of the slice: x: 2, y: 2, z: 4, core: 2. Of those that a mesh axis runs over, the one named last changes fastest.
Arguments:
- grad_out: bfloat16 [1024, 4096], P('expert', 'tensor'), may hold values from -6 to 6
- expert_ids: int32 [1024, 4], P('expert'), may hold values from 0 to 7, all different within a row
- gate_probs: float32 [1024, 4], P('expert'), may hold values from 0.05 to 0.6
- live: int32 [1024], P('expert'), may hold values 0 or 1
- w_gate: bfloat16 [8, 5376, 4096], P('expert', 'tensor'), may hold values from -0.09375 to 0.09375
- w_up: bfloat16 [8, 5376, 4096], P('expert', 'tensor'), may hold values from -0.09375 to 0.09375
- w_down: bfloat16 [8, 5376, 4096], P('expert', 'tensor'), may hold values from -0.078125 to 0.078125
- saved: bfloat16 [8, 2, 5376, 512], P('expert', None, 'tensor'), may hold values from -8 to 8
Outputs:
- grad_in: bfloat16 [1024, 4096], P('expert', 'tensor')
The draws below stay inside these ranges and needn't reach their ends.
Inputs may be any that keep to these rules, and one draw needn't show every extreme that they name: `expert_ids`: the 4 ids of a token are different.
All inputs are finite; a program needn't handle non-finite values. No bound on the sum of `live` on one device may be relied on, other than what follows from the above.
Results may differ from the reference program's by a relative error of at most 0.012.
Values may be sent and summed in bfloat16 or wider, within the bound.
A program may use at most 128 MiB of HBM per device.

```python
import math
import jax
import jax.numpy as jnp
from jax import lax

D = 4096
FF = 5376
TOP = 4
TOK_G = 128
TOKENS = 1024
EXPERTS = 8
CAP = 64
SLOTS = 512
N_EXPERT = 8
N_TENSOR = 4


def place_ends(array, own_key, low, top_value):
    longest = array.shape.index(max(array.shape))
    spots = []
    for shift in (0, 1):
        where = [jax.random.randint(jax.random.fold_in(own_key, axis), (), 0, length) for axis, length in enumerate(array.shape)]
        where[longest] = (where[longest] + shift) % array.shape[longest]
        spots.append(tuple(where))
    return array.at[spots[0]].set(low).at[spots[1]].set(top_value)


def level_of(stream_key, dims, cuts, least, largest):
    gain, own = 1.0, jax.random.fold_in(stream_key, 6)
    for dim, blocks in cuts:
        steps = jnp.exp(jax.random.uniform(jax.random.fold_in(own, dim), (blocks,), jnp.float32, least / len(cuts), largest / len(cuts)))
        gain = gain * jnp.repeat(steps, dims[dim] // blocks).reshape([-1 if axis == dim else 1 for axis in range(len(dims))])
    return gain


def distinct(stream_key, rows, number_of, top, lift):
    ranking = jax.random.permutation(jax.random.fold_in(stream_key, 1), number_of)
    pull = ranking
    for power in range(3):
        pull = pull * pull // number_of
    pull = pull * lift // number_of
    tickets = jax.random.randint(jax.random.fold_in(stream_key, 2), (rows, number_of), 0, 4096) + pull
    sure = jax.random.permutation(jax.random.fold_in(stream_key, 3), rows)[jnp.arange(number_of) % rows]
    tickets = jnp.where(jnp.arange(rows)[:, None] == sure[None, :], 1 << 14, tickets)
    merit = tickets * number_of + jnp.arange(number_of)
    return lax.top_k(merit.astype(jnp.int32), top)[1].astype(jnp.int32)


def scatter_about(own_key, shape, spread, most, split=(), kind=jnp.bfloat16):
    drawn = jax.random.normal(own_key, shape, jnp.float32) * spread
    if len(split) > 0:
        drawn = level_of(own_key, shape, split, -0.22, 0.18) * drawn
    return jnp.clip(drawn, min=-most, max=most).astype(kind)


def setup_inputs(seed: int = 0) -> dict:
    streams_of = jax.random.split(jax.random.key(seed), 9)
    return {
        "grad_out": scatter_about(streams_of[0], (TOKENS, D), 1.0, 6.0, ((0, 8), (1, 4))),
        "expert_ids": distinct(streams_of[1], TOKENS, EXPERTS, TOP, 8192),
        "gate_probs": jnp.clip(jnp.exp(math.log(0.6) - 2.4849067 * jax.random.uniform(streams_of[2], (TOKENS, TOP), jnp.float32) ** level_of(streams_of[2], (TOKENS, TOP), ((0, 8),), -0.2, 0.2)), 0.05, 0.6),
        "live": place_ends((jax.random.randint(streams_of[3], (TOKENS,), 0, 8) < 7).astype(jnp.int32), jax.random.fold_in(streams_of[3], 1), 0, 1),
        "w_gate": scatter_about(streams_of[4], (EXPERTS, FF, D), D ** -0.5, 0.09375, ((0, 8), (1, 4))),
        "w_up": scatter_about(streams_of[5], (EXPERTS, FF, D), D ** -0.5, 0.09375, ((0, 8), (1, 4))),
        "w_down": scatter_about(streams_of[6], (EXPERTS, FF, D), FF ** -0.5, 0.078125, ((0, 8), (1, 4))),
        "saved": scatter_about(streams_of[7], (EXPERTS, 2, FF, SLOTS), 1.5, 8.0, ((0, 8), (2, 4))),
    }


def reference(grad_out, expert_ids, gate_probs, live, w_gate, w_up, w_down, saved):
    groups = N_EXPERT
    experts = EXPERTS
    ids = expert_ids.reshape(groups, TOK_G * TOP)
    alive = jnp.repeat(live.reshape(groups, TOK_G), TOP, axis=1)
    onehot = (ids[:, :, None] == jnp.arange(experts, dtype=jnp.int32)[None, None, :]).astype(jnp.int32) * alive[:, :, None]
    position = jnp.sum((jnp.cumsum(onehot, axis=1) - onehot) * onehot, axis=2)
    kept = (jnp.sum(onehot, axis=2) > 0) & (position < CAP)
    group_index = jnp.arange(groups, dtype=jnp.int32)[:, None]
    place = ids * SLOTS + group_index * CAP + position
    place = jnp.where(kept, place, experts * SLOTS).astype(jnp.int32)
    scaled = (gate_probs.reshape(groups, TOK_G, TOP, 1) * grad_out.reshape(groups, TOK_G, 1, D).astype(jnp.float32)).astype(jnp.bfloat16)
    scaled = scaled.reshape(groups * TOK_G * TOP, D)
    buffer = jnp.zeros((experts * SLOTS + 1, D), jnp.bfloat16).at[place.reshape(-1)].set(scaled)
    buffer = buffer[: experts * SLOTS].reshape(experts, SLOTS, D)
    block_width = FF // N_TENSOR

    def one_expert(index):
        rows = buffer[index]
        grad_hidden = jnp.dot(w_down[index], rows.T, preferred_element_type=jnp.float32)
        pre_gate = saved[index, 0].astype(jnp.float32)
        pre_up = saved[index, 1].astype(jnp.float32)
        sigma = jax.nn.sigmoid(pre_gate)
        d_up = (grad_hidden * pre_gate * sigma).astype(jnp.bfloat16)
        d_gate = (grad_hidden * pre_up * sigma * (1.0 + pre_gate * (1.0 - sigma))).astype(jnp.bfloat16)
        gate_rows = w_gate[index]
        up_rows = w_up[index]

        def block(total, number):
            low = number * block_width
            gate_part = lax.dynamic_slice_in_dim(d_gate, low, block_width, 0)
            up_part = lax.dynamic_slice_in_dim(d_up, low, block_width, 0)
            gate_weights = lax.dynamic_slice_in_dim(gate_rows, low, block_width, 0)
            up_weights = lax.dynamic_slice_in_dim(up_rows, low, block_width, 0)
            term = jnp.dot(gate_part.T, gate_weights, preferred_element_type=jnp.float32)
            term = term + jnp.dot(up_part.T, up_weights, preferred_element_type=jnp.float32)
            rounded = lax.optimization_barrier(term.astype(jnp.bfloat16))
            return total + rounded.astype(jnp.float32), None

        total, _ = lax.scan(block, jnp.zeros((SLOTS, D), jnp.float32), jnp.arange(N_TENSOR, dtype=jnp.int32))
        return total

    slot_grad = lax.map(one_expert, jnp.arange(experts, dtype=jnp.int32))
    flat_rows = slot_grad.reshape(experts * SLOTS, D)
    picked = flat_rows[jnp.minimum(place, experts * SLOTS - 1).reshape(-1)]
    picked = picked * kept.reshape(-1, 1).astype(jnp.float32)
    grad_in = jnp.sum(picked.reshape(groups * TOK_G, TOP, D), axis=1)
    return grad_in.astype(jnp.bfloat16)
```

```python
import functools

import jax
import jax.numpy as jnp
from jax import lax
from jax.experimental import pallas as pl
from jax.experimental.pallas import tpu as pltpu
from jax.sharding import PartitionSpec as P

MESH = pl.DeviceIdType.MESH
NT = (((1,), (1,)), ((), ()))
NN = (((1,), (0,)), ((), ()))


def dot(a, b, dims):
    return lax.dot_general(a, b, dims, preferred_element_type=jnp.float32)


def mate(me, step, size, sign):
    if size & (size - 1):
        return lax.rem(me + (sign * step) % size, size)
    out, bit = 0, 1
    while bit < size:
        mine = lax.rem(lax.div(me, bit), 2)
        out = out + (1 - mine if step & bit else mine) * bit
        bit *= 2
    return out


def shortcuts(nt, pieces):
    ahead = [0] * nt
    for s, share in ((1, 2), (2, 4)):
        if s < nt:
            ahead[s] = pieces // share
    return ahead


def kernel(
    ne, nt, cap, raw0, ids, gates, live, w_gate, w_up, w_down, saved, out,
    wd, wg, wu, sv, svt, dh, sel, gs, back, outgoing, recv, orecv, raw, part, zrecv, zterm,
    w_sem, sv_sem, in_send, in_recv, out_send, out_recv, z_send, z_recv, p_send, p_recv,
    b_send, t_send, t_recv,
):
    me = lax.axis_index("expert")
    mz = lax.axis_index("tensor")
    tokens, chunk = raw0.shape
    slots = ne * cap
    hidden = saved.shape[2]
    tops = ids.shape[0]
    steps = range(nt)
    owner = [mate(mz, s, nt, 1) for s in steps]
    zpeer = [mate(mz, s, nt, -1) for s in steps]
    order = sorted(range(1, ne), key=lambda j: (-(j // 2) if j > 1 else 1, j))
    epeer = [mate(me, j, ne, 1) for j in order]

    barrier = pltpu.get_barrier_semaphore()
    for peer in epeer:
        pl.semaphore_signal(barrier, inc=1, device_id=(peer, mz), device_id_type=MESH)
    for s in range(1, nt):
        pl.semaphore_signal(barrier, inc=1, device_id=(me, zpeer[s]), device_id_type=MESH)

    def weight_copy(i, s):
        src = (w_down, w_gate, w_up)[i]
        dst = (wd, wg, wu)[i]
        columns = pl.ds(pl.multiple_of(owner[s] * chunk, chunk), chunk)
        return pltpu.make_async_copy(src.at[0, :, columns], dst.at[s], w_sem.at[i, s])

    saved_copy = pltpu.make_async_copy(saved.at[0], sv, sv_sem.at[0])

    experts = lax.broadcasted_iota(jnp.int32, (ne, tokens), 0)
    alive = live[...] != 0
    chosen = jnp.zeros((ne, tokens), jnp.float32)
    weight = jnp.zeros((ne, tokens), jnp.float32)
    for k in range(tops):
        match = (ids[k : k + 1, :] == experts) & alive
        chosen = chosen + jnp.where(match, 1.0, 0.0)
        weight = weight + jnp.where(match, gates[k : k + 1, :], 0.0)
    row = lax.broadcasted_iota(jnp.int32, (tokens, tokens), 0)
    col = lax.broadcasted_iota(jnp.int32, (tokens, tokens), 1)
    before = jnp.where(row < col, 1.0, 0.0).astype(jnp.bfloat16)
    position = dot(chosen.astype(jnp.bfloat16), before, NN)
    position = jnp.where((chosen > 0.0) & (position < cap), position, -1.0)
    slot = lax.broadcasted_iota(jnp.int32, (cap, tokens), 0).astype(jnp.float32)
    for e in range(ne):
        hit = slot == position[e : e + 1, :]
        sel[e * cap : (e + 1) * cap, :] = jnp.where(hit, 1.0, 0.0).astype(jnp.bfloat16)
        gate = jnp.sum(jnp.where(hit, weight[e : e + 1, :], 0.0), axis=1, keepdims=True)
        gs[e * cap : (e + 1) * cap, :] = jnp.broadcast_to(gate, (cap, gs.shape[1]))

    tile = min(256, chunk)
    pieces = chunk // tile
    ahead = shortcuts(nt, pieces)
    crossing = [(s, j) for s in steps for j in range(ahead[s])]

    def piece(j):
        return pl.ds(pl.multiple_of(j * tile, tile), tile)

    def build(src, s, j):
        picked = dot(sel[...], src[:, piece(j)], NN)
        outgoing[s, :, piece(j)] = (gs[:, :1] * picked).astype(jnp.bfloat16)

    def rows(e):
        return pl.ds(pl.multiple_of(e * cap, cap), cap)

    def exchange(s, j, dst, send, receive):
        for peer in epeer:
            pltpu.make_async_remote_copy(
                src_ref=outgoing.at[s, rows(peer), piece(j)],
                dst_ref=dst.at[s, rows(me), piece(j)],
                send_sem=send.at[s, j],
                recv_sem=receive.at[s, j],
                device_id=(peer, mz),
                device_id_type=MESH,
            ).start()
        pltpu.make_async_copy(
            outgoing.at[s, rows(me), piece(j)],
            dst.at[s, rows(me), piece(j)],
            receive.at[s, j],
        ).start()

    def wait_all(ref, sem):
        pltpu.make_async_copy(ref, ref, sem).wait()

    def z_copy(src, dst, send, receive, peer):
        return pltpu.make_async_remote_copy(
            src_ref=src,
            dst_ref=dst,
            send_sem=send,
            recv_sem=receive,
            device_id=(me, peer),
            device_id_type=MESH,
        )

    def beyond(s):
        return pl.ds(ahead[s] * tile, chunk - ahead[s] * tile)

    pl.semaphore_wait(barrier, ne - 1 + nt - 1)
    z_copies = {
        s: z_copy(
            raw0.at[:, beyond(s)], raw.at[s, :, beyond(s)], z_send.at[s], z_recv.at[s], zpeer[s]
        )
        for s in range(1, nt)
    }
    for copy in z_copies.values():
        copy.start()

    def give(src, s):
        @pl.loop(ahead[s], pieces)
        def _(j):
            build(src, s, j)
            exchange(s, j, recv, in_send, in_recv)

    give(raw0, 0)

    saved_copy.start()
    for s in steps:
        weight_copy(0, s).start()
    for s in reversed(steps):
        weight_copy(1, s).start()
        weight_copy(2, s).start()

    shared = {
        (s, j): z_copy(
            recv.at[0, :, piece(j)], recv.at[s, :, piece(j)], b_send.at[k], in_recv.at[s, j], zpeer[s]
        )
        for k, (s, j) in enumerate(crossing)
    }
    for s in range(1, nt):
        z_copies[s].wait_recv()
        give(raw.at[s], s)
        if s == 1:
            for j in range(max(ahead)):
                wait_all(recv.at[0, :, piece(j)], in_recv.at[0, j])
                for q in range(1, nt):
                    if j < ahead[q]:
                        shared[q, j].start()

    row = lax.broadcasted_iota(jnp.int32, (tokens, tokens), 0)
    col = lax.broadcasted_iota(jnp.int32, (tokens, tokens), 1)
    eye = jnp.where(row == col, 1.0, 0.0).astype(jnp.bfloat16)
    back[...] = dot(eye, sel[...], NT).astype(jnp.bfloat16)
    block = min(128, slots)
    saved_copy.wait()

    @pl.loop(0, slots // block)
    def _(b):
        at = pl.ds(pl.multiple_of(b * block, block), block)
        r = lax.broadcasted_iota(jnp.int32, (block, block), 0)
        c = lax.broadcasted_iota(jnp.int32, (block, block), 1)
        one = jnp.where(r == c, 1.0, 0.0).astype(jnp.bfloat16)
        for i in range(2):
            svt[i, at, :] = dot(one, sv[i, :, at], NT).astype(jnp.bfloat16)

    half = min(256, slots)
    for s in steps:
        weight_copy(0, s).wait()
        for j in range(0 if s > 0 or nt == 1 else max(ahead), pieces):
            wait_all(recv.at[s, :, piece(j)], in_recv.at[s, j])

        @pl.loop(0, slots // half)
        def _(b):
            at = pl.ds(pl.multiple_of(b * half, half), half)
            part_sum = dot(recv[s, at, :], wd[s], NT)
            if s == 0:
                dh[at, :] = part_sum
            else:
                dh[at, :] = dh[at, :] + part_sum

    few = 16

    @pl.loop(0, slots // few)
    def _(b):
        at = pl.ds(pl.multiple_of(b * few, few), few)
        grad = dh[at, :]
        a = svt[0, at, :].astype(jnp.float32)
        u = svt[1, at, :].astype(jnp.float32)
        sig = jax.nn.sigmoid(a)
        svt[1, at, :] = (grad * a * sig).astype(jnp.bfloat16)
        svt[0, at, :] = (grad * u * sig * (1.0 + a * (1.0 - sig))).astype(jnp.bfloat16)

    def combine(s, j):
        return dot(back[...], orecv[s, :, piece(j)], NN)

    p_copies = {
        s: z_copy(
            part.at[s, :, beyond(s)], zrecv.at[s, :, beyond(s)], p_send.at[s], p_recv.at[s], owner[s]
        )
        for s in range(1, nt)
    }
    t_copies = {
        (s, j): z_copy(
            outgoing.at[s, :, piece(j)], zterm.at[k], t_send.at[k], t_recv.at[k], owner[s]
        )
        for k, (s, j) in enumerate(crossing)
    }
    others = outgoing.at[0, pl.ds(0, (ne - 1) * cap), pl.ds(0, tile)]

    def term(s, j):
        total = dot(svt[0], wg[s, :, piece(j)], NN)
        return total + dot(svt[1], wu[s, :, piece(j)], NN)

    def hand(s, low, high):
        @pl.loop(low, high)
        def _(j):
            wait_all(others, in_send.at[s, j])
            outgoing[s, :, piece(j)] = term(s, j).astype(jnp.bfloat16)
            exchange(s, j, orecv, out_send, out_recv)

    def hand_across(s):
        for j in range(ahead[s]):
            outgoing[s, :, piece(j)] = term(s, j).astype(jnp.bfloat16)
            t_copies[s, j].start()

    def weights_of(s):
        weight_copy(1, s).wait()
        weight_copy(2, s).wait()

    last = nt - 1
    lead = ahead[last] if last == 0 else min(ahead[last] + 1, pieces)
    if last > 0:
        weights_of(last)
        hand(last, ahead[last], lead)
        for s in range(1, nt):
            if ahead[s] > 0:
                if s < last:
                    weights_of(s)
                hand_across(s)
        hand(last, lead, pieces)
    for s in reversed(range(1, last)):
        if ahead[s] == 0:
            weights_of(s)
        hand(s, ahead[s], pieces)
    weights_of(0)
    hand(0, max(ahead), pieces)
    for j in reversed(range(max(ahead))):
        total = term(0, j)
        for k, (s, q) in enumerate(crossing):
            if q == j:
                t_copies[s, q].wait_recv()
                total = total + zterm[k].astype(jnp.float32)
        wait_all(others, in_send.at[0, j])
        outgoing[0, :, piece(j)] = total.astype(jnp.bfloat16)
        exchange(0, j, orecv, out_send, out_recv)

    for s in reversed(range(1, nt)):

        @pl.loop(ahead[s], pieces)
        def _(j):
            wait_all(orecv.at[s, :, piece(j)], out_recv.at[s, j])
            part[s, :, piece(j)] = combine(s, j).astype(jnp.bfloat16)

        p_copies[s].start()
    for s in range(1, nt):
        p_copies[s].wait_recv()
    for j in [*range(max(ahead), pieces), *reversed(range(max(ahead)))]:
        wait_all(orecv.at[0, :, piece(j)], out_recv.at[0, j])
        total = combine(0, j)
        for q in range(1, nt):
            if j >= ahead[q]:
                total = total + zrecv[q, :, piece(j)].astype(jnp.float32)
        out[:, piece(j)] = total.astype(jnp.bfloat16)

    for s in steps:
        for j in range(ahead[s], pieces):
            wait_all(others, out_send.at[s, j])
    for s in range(1, nt):
        z_copies[s].wait_send()
        p_copies[s].wait_send()
    for pair in crossing:
        shared[pair].wait_send()
        t_copies[pair].wait_send()


def shards(grad_out, expert_ids, gate_probs, live, w_gate, w_up, w_down, saved):
    ne = lax.axis_size("expert")
    nt = lax.axis_size("tensor")
    tokens, chunk = grad_out.shape
    cap = tokens * expert_ids.shape[1] // ne
    slots = ne * cap
    hidden = saved.shape[2]
    tile = min(256, chunk)
    pieces = chunk // tile
    crossings = max(1, sum(shortcuts(nt, pieces)))
    bf16, f32 = jnp.bfloat16, jnp.float32
    vmem = pl.BlockSpec(memory_space=pltpu.VMEM)
    anywhere = pl.BlockSpec(memory_space=pl.ANY)
    dma = pltpu.SemaphoreType.DMA
    return pl.pallas_call(
        functools.partial(kernel, ne, nt, cap),
        out_shape=jax.ShapeDtypeStruct((tokens, chunk), bf16),
        in_specs=[vmem] * 4 + [anywhere] * 4,
        out_specs=vmem,
        scratch_shapes=[
            pltpu.VMEM((nt, hidden, chunk), bf16),
            pltpu.VMEM((nt, hidden, chunk), bf16),
            pltpu.VMEM((nt, hidden, chunk), bf16),
            pltpu.VMEM((2, hidden, slots), bf16),
            pltpu.VMEM((2, slots, hidden), bf16),
            pltpu.VMEM((slots, hidden), f32),
            pltpu.VMEM((slots, tokens), bf16),
            pltpu.VMEM((slots, 128), f32),
            pltpu.VMEM((tokens, slots), bf16),
            pltpu.VMEM((nt, slots, chunk), bf16),
            pltpu.VMEM((nt, slots, chunk), bf16),
            pltpu.VMEM((nt, slots, chunk), bf16),
            pltpu.VMEM((nt, tokens, chunk), bf16),
            pltpu.VMEM((nt, tokens, chunk), bf16),
            pltpu.VMEM((nt, tokens, chunk), bf16),
            pltpu.VMEM((crossings, slots, tile), bf16),
            dma((3, nt)),
            dma((1,)),
            dma((nt, pieces)),
            dma((nt, pieces)),
            dma((nt, pieces)),
            dma((nt, pieces)),
            dma((nt,)),
            dma((nt,)),
            dma((nt,)),
            dma((nt,)),
            dma((crossings,)),
            dma((crossings,)),
            dma((crossings,)),
        ],
        compiler_params=pltpu.CompilerParams(
            collective_id=0, has_side_effects=True, vmem_limit_bytes=67043328
        ),
    )(
        grad_out,
        expert_ids.T,
        gate_probs.T,
        live.reshape(1, tokens),
        w_gate,
        w_up,
        w_down,
        saved,
    )


def solution(mesh):
    placed = (
        P("expert", "tensor"),
        P("expert", None),
        P("expert", None),
        P("expert"),
        P("expert", "tensor", None),
        P("expert", "tensor", None),
        P("expert", "tensor", None),
        P("expert", None, "tensor", None),
    )
    return jax.shard_map(
        shards, mesh=mesh, in_specs=placed, out_specs=P("expert", "tensor"), check_vma=False
    )
```

```python
import functools

import jax
import jax.numpy as jnp
from jax import lax
from jax.experimental import pallas as pl
from jax.experimental.pallas import tpu as pltpu
from jax.sharding import PartitionSpec as P

MESH = pl.DeviceIdType.MESH
NT = (((1,), (1,)), ((), ()))
NN = (((1,), (0,)), ((), ()))


def dot(a, b, dims):
    return lax.dot_general(a, b, dims, preferred_element_type=jnp.float32)


def mate(me, step, size, sign):
    if size & (size - 1):
        return lax.rem(me + (sign * step) % size, size)
    out, bit = 0, 1
    while bit < size:
        mine = lax.rem(lax.div(me, bit), 2)
        out = out + (1 - mine if step & bit else mine) * bit
        bit *= 2
    return out


INWARD = ((1, 2), (2, 1))
OUTWARD = ((1, 2), (2, 1))


def shortcuts(nt, pieces, shares):
    across = [0] * nt
    for s, quarters in shares:
        if s < nt:
            across[s] = pieces * quarters // 4
    return across


def kernel(
    ne, nt, cap, raw0, ids, gates, live, w_gate, w_up, w_down, saved, out,
    wd, wg, wu, sv, svt, dh, sel, gs, back, outgoing, recv, orecv, raw, part, zrecv, zterm,
    w_sem, sv_sem, in_send, in_recv, out_send, out_recv, z_send, z_recv, p_send, p_recv,
    b_send, t_send, t_recv,
):
    me = lax.axis_index("expert")
    mz = lax.axis_index("tensor")
    tokens, chunk = raw0.shape
    slots = ne * cap
    hidden = saved.shape[2]
    tops = ids.shape[0]
    steps = range(nt)
    owner = [mate(mz, s, nt, 1) for s in steps]
    zpeer = [mate(mz, s, nt, -1) for s in steps]
    order = sorted(range(1, ne), key=lambda j: (-(j // 2) if j > 1 else 1, j))
    epeer = [mate(me, j, ne, 1) for j in order]

    barrier = pltpu.get_barrier_semaphore()
    for peer in epeer:
        pl.semaphore_signal(barrier, inc=1, device_id=(peer, mz), device_id_type=MESH)
    for s in range(1, nt):
        pl.semaphore_signal(barrier, inc=1, device_id=(me, zpeer[s]), device_id_type=MESH)

    def weight_copy(i, s):
        src = (w_down, w_gate, w_up)[i]
        dst = (wd, wg, wu)[i]
        columns = pl.ds(pl.multiple_of(owner[s] * chunk, chunk), chunk)
        return pltpu.make_async_copy(src.at[0, :, columns], dst.at[s], w_sem.at[i, s])

    saved_copy = pltpu.make_async_copy(saved.at[0], sv, sv_sem.at[0])

    tile = min(256, chunk)
    pieces = chunk // tile
    ahead = shortcuts(nt, pieces, INWARD)
    astern = shortcuts(nt, pieces, OUTWARD)
    halves = range(2)
    part_cap, part_slots = cap // 2, slots // 2

    def crossings(across):
        return [(s, j, h) for h in halves for j in range(max(across)) for s in steps if j < across[s]]

    def span(h):
        return pl.ds(h * part_slots, part_slots)

    def piece(j):
        return pl.ds(pl.multiple_of(j * tile, tile), tile)

    def build(src, s, j, h):
        picked = dot(sel[span(h), :], src[:, piece(j)], NN)
        outgoing[s, span(h), piece(j)] = (gs[span(h), :1] * picked).astype(jnp.bfloat16)

    def rows(h, e):
        return pl.ds(pl.multiple_of(h * part_slots + e * part_cap, part_cap), part_cap)

    def exchange(s, j, h, dst, send, receive):
        for peer in epeer:
            pltpu.make_async_remote_copy(
                src_ref=outgoing.at[s, rows(h, peer), piece(j)],
                dst_ref=dst.at[s, rows(h, me), piece(j)],
                send_sem=send.at[s, j, h],
                recv_sem=receive.at[s, j, h],
                device_id=(peer, mz),
                device_id_type=MESH,
            ).start()
        pltpu.make_async_copy(
            outgoing.at[s, rows(h, me), piece(j)],
            dst.at[s, rows(h, me), piece(j)],
            receive.at[s, j, h],
        ).start()

    def wait_all(ref, sem):
        pltpu.make_async_copy(ref, ref, sem).wait()

    def z_copy(src, dst, send, receive, peer):
        return pltpu.make_async_remote_copy(
            src_ref=src,
            dst_ref=dst,
            send_sem=send,
            recv_sem=receive,
            device_id=(me, peer),
            device_id_type=MESH,
        )

    def beyond(s, across):
        return pl.ds(across[s] * tile, chunk - across[s] * tile)

    pl.semaphore_wait(barrier, ne - 1 + nt - 1)
    z_copies = {
        s: z_copy(
            raw0.at[:, beyond(s, ahead)],
            raw.at[s, :, beyond(s, ahead)],
            z_send.at[s],
            z_recv.at[s],
            zpeer[s],
        )
        for s in range(1, nt)
    }
    for copy in z_copies.values():
        copy.start()

    experts = lax.broadcasted_iota(jnp.int32, (ne, tokens), 0)
    alive = live[...] != 0
    chosen = jnp.zeros((ne, tokens), jnp.float32)
    weight = jnp.zeros((ne, tokens), jnp.float32)
    for k in range(tops):
        match = (ids[k : k + 1, :] == experts) & alive
        chosen = chosen + jnp.where(match, 1.0, 0.0)
        weight = weight + jnp.where(match, gates[k : k + 1, :], 0.0)
    row = lax.broadcasted_iota(jnp.int32, (tokens, tokens), 0)
    col = lax.broadcasted_iota(jnp.int32, (tokens, tokens), 1)
    before = jnp.where(row < col, 1.0, 0.0).astype(jnp.bfloat16)
    position = dot(chosen.astype(jnp.bfloat16), before, NN)
    position = jnp.where((chosen > 0.0) & (position < cap), position, -1.0)
    slot = lax.broadcasted_iota(jnp.int32, (cap, tokens), 0).astype(jnp.float32)
    for e in range(ne):
        hit = slot == position[e : e + 1, :]
        gate = jnp.sum(jnp.where(hit, weight[e : e + 1, :], 0.0), axis=1, keepdims=True)
        gate = jnp.broadcast_to(gate, (cap, gs.shape[1]))
        hit = jnp.where(hit, 1.0, 0.0)
        for h in halves:
            some = slice(h * part_cap, (h + 1) * part_cap)
            sel[rows(h, e), :] = hit[some].astype(jnp.bfloat16)
            gs[rows(h, e), :] = gate[some]

    def give(src, s, which):
        @pl.loop(ahead[s], pieces)
        def _(j):
            for h in which:
                build(src, s, j, h)
                exchange(s, j, h, recv, in_send, in_recv)

    give(raw0, 0, halves)

    saved_copy.start()
    for s in steps:
        weight_copy(0, s).start()
    for s in reversed(steps):
        weight_copy(1, s).start()
        weight_copy(2, s).start()

    shared = {
        (s, j, h): z_copy(
            recv.at[0, span(h), piece(j)],
            recv.at[s, span(h), piece(j)],
            b_send.at[k],
            in_recv.at[s, j, h],
            zpeer[s],
        )
        for k, (s, j, h) in enumerate(crossings(ahead))
    }

    def landed(dst, s, j, h, receive):
        wait_all(dst.at[s, span(h), piece(j)], receive.at[s, j, h])

    early = max(1, nt // 2)
    for s in range(1, nt):
        z_copies[s].wait_recv()
        give(raw.at[s], s, halves if s < early else [0])
        if s == 1:
            for h in halves:
                for j in range(max(ahead)):
                    landed(recv, 0, j, h, in_recv)
            for copy in shared.values():
                copy.start()
    for s in range(early, nt):
        give(raw.at[s], s, [1])

    row = lax.broadcasted_iota(jnp.int32, (tokens, tokens), 0)
    col = lax.broadcasted_iota(jnp.int32, (tokens, tokens), 1)
    eye = jnp.where(row == col, 1.0, 0.0).astype(jnp.bfloat16)
    back[...] = dot(eye, sel[...], NT).astype(jnp.bfloat16)
    block = max(cap, min(128, slots))
    saved_copy.wait()

    @pl.loop(0, slots // block)
    def _(b):
        at = pl.ds(pl.multiple_of(b * block, block), block)
        r = lax.broadcasted_iota(jnp.int32, (block, block), 0)
        c = lax.broadcasted_iota(jnp.int32, (block, block), 1)
        one = jnp.where(r == c, 1.0, 0.0).astype(jnp.bfloat16)
        for i in range(2):
            turned = dot(one, sv[i, :, at], NT).astype(jnp.bfloat16)
            for g in range(block // cap):
                for h in halves:
                    some = slice(g * cap + h * part_cap, g * cap + (h + 1) * part_cap)
                    svt[i, rows(h, b * (block // cap) + g), :] = turned[some]

    def contract(s, h):
        for j in range(pieces):
            if s > 0 or nt == 1 or j >= max(ahead):
                landed(recv, s, j, h, in_recv)
        part_sum = dot(recv[s, span(h), :], wd[s], NT)
        dh[span(h), :] = part_sum if s == 0 else dh[span(h), :] + part_sum

    few = 16

    def activate(h):
        @pl.loop(h * part_slots // few, (h + 1) * part_slots // few)
        def _(b):
            at = pl.ds(pl.multiple_of(b * few, few), few)
            grad = dh[at, :]
            a = svt[0, at, :].astype(jnp.float32)
            u = svt[1, at, :].astype(jnp.float32)
            sig = jax.nn.sigmoid(a)
            svt[1, at, :] = (grad * a * sig).astype(jnp.bfloat16)
            svt[0, at, :] = (grad * u * sig * (1.0 + a * (1.0 - sig))).astype(jnp.bfloat16)

    def combine(s, j):
        return dot(back[...], orecv[s, :, piece(j)], NN)

    p_copies = {
        s: z_copy(
            part.at[s, :, beyond(s, astern)],
            zrecv.at[s, :, beyond(s, astern)],
            p_send.at[s],
            p_recv.at[s],
            owner[s],
        )
        for s in range(1, nt)
    }
    t_copies = {
        (s, j, h): z_copy(
            outgoing.at[s, span(h), piece(j)], zterm.at[k], t_send.at[k], t_recv.at[k], owner[s]
        )
        for k, (s, j, h) in enumerate(crossings(astern))
    }
    others = outgoing.at[0, pl.ds(0, (ne - 1) * part_cap), pl.ds(0, tile)]

    def term(s, j, h):
        total = dot(svt[0, span(h), :], wg[s, :, piece(j)], NN)
        return total + dot(svt[1, span(h), :], wu[s, :, piece(j)], NN)

    def vacant(s, j, h):
        wait_all(others, in_send.at[s, j, h])

    def hand(s, h, low, high):
        @pl.loop(low, high)
        def _(j):
            vacant(s, j, h)
            outgoing[s, span(h), piece(j)] = term(s, j, h).astype(jnp.bfloat16)
            exchange(s, j, h, orecv, out_send, out_recv)

    def hand_across(s, h):
        for j in range(astern[s]):
            if j >= ahead[s]:
                vacant(s, j, h)
            outgoing[s, span(h), piece(j)] = term(s, j, h).astype(jnp.bfloat16)
            t_copies[s, j, h].start()

    last = nt - 1

    def send_back_own(h):
        for j in reversed(range(max(astern))):
            total = term(0, j, h)
            for k, (s, q, half) in enumerate(crossings(astern)):
                if q == j and half == h:
                    t_copies[s, q, h].wait_recv()
                    total = total + zterm[k].astype(jnp.float32)
            vacant(0, j, h)
            outgoing[0, span(h), piece(j)] = total.astype(jnp.bfloat16)
            exchange(0, j, h, orecv, out_send, out_recv)

    for s in steps:
        weight_copy(0, s).wait()
        contract(s, 0)
        if s == 0:
            contract(s, 1)
    activate(0)
    for s in steps:
        weight_copy(1, s).wait()
        weight_copy(2, s).wait()
    hand(0, 0, max(astern), pieces)
    for s in range(1, nt):
        hand_across(s, 0)
    for s in [*range(1, early), *([last] if last >= early else [])]:
        hand(s, 0, astern[s], pieces)
    for s in range(1, nt):
        contract(s, 1)
    activate(1)
    for s in reversed(range(early, nt)):
        if s < last:
            hand(s, 0, astern[s], pieces)
        hand(s, 1, astern[s], pieces)
        if s == last:
            for q in range(1, nt):
                hand_across(q, 1)
    for s in reversed(range(1, early)):
        hand(s, 1, astern[s], pieces)
    send_back_own(0)
    hand(0, 1, max(astern), pieces)
    send_back_own(1)

    for s in reversed(range(1, nt)):

        @pl.loop(astern[s], pieces)
        def _(j):
            for h in halves:
                landed(orecv, s, j, h, out_recv)
            part[s, :, piece(j)] = combine(s, j).astype(jnp.bfloat16)

        p_copies[s].start()
    for s in range(1, nt):
        p_copies[s].wait_recv()
    for j in [*range(max(astern), pieces), *reversed(range(max(astern)))]:
        for h in halves:
            landed(orecv, 0, j, h, out_recv)
        total = combine(0, j)
        for q in range(1, nt):
            if j >= astern[q]:
                total = total + zrecv[q, :, piece(j)].astype(jnp.float32)
        out[:, piece(j)] = total.astype(jnp.bfloat16)

    for s in steps:
        for j in range(pieces):
            for h in halves:
                if j >= astern[s]:
                    wait_all(others, out_send.at[s, j, h])
    for s in range(1, nt):
        z_copies[s].wait_send()
        p_copies[s].wait_send()
    for copy in [*shared.values(), *t_copies.values()]:
        copy.wait_send()


def shards(grad_out, expert_ids, gate_probs, live, w_gate, w_up, w_down, saved):
    ne = lax.axis_size("expert")
    nt = lax.axis_size("tensor")
    tokens, chunk = grad_out.shape
    cap = tokens * expert_ids.shape[1] // ne
    slots = ne * cap
    hidden = saved.shape[2]
    tile = min(256, chunk)
    pieces = chunk // tile
    inward = max(1, 2 * sum(shortcuts(nt, pieces, INWARD)))
    outward = max(1, 2 * sum(shortcuts(nt, pieces, OUTWARD)))
    bf16, f32 = jnp.bfloat16, jnp.float32
    vmem = pl.BlockSpec(memory_space=pltpu.VMEM)
    anywhere = pl.BlockSpec(memory_space=pl.ANY)
    dma = pltpu.SemaphoreType.DMA
    return pl.pallas_call(
        functools.partial(kernel, ne, nt, cap),
        out_shape=jax.ShapeDtypeStruct((tokens, chunk), bf16),
        in_specs=[vmem] * 4 + [anywhere] * 4,
        out_specs=vmem,
        scratch_shapes=[
            pltpu.VMEM((nt, hidden, chunk), bf16),
            pltpu.VMEM((nt, hidden, chunk), bf16),
            pltpu.VMEM((nt, hidden, chunk), bf16),
            pltpu.VMEM((2, hidden, slots), bf16),
            pltpu.VMEM((2, slots, hidden), bf16),
            pltpu.VMEM((slots, hidden), f32),
            pltpu.VMEM((slots, tokens), bf16),
            pltpu.VMEM((slots, 128), f32),
            pltpu.VMEM((tokens, slots), bf16),
            pltpu.VMEM((nt, slots, chunk), bf16),
            pltpu.VMEM((nt, slots, chunk), bf16),
            pltpu.VMEM((nt, slots, chunk), bf16),
            pltpu.VMEM((nt, tokens, chunk), bf16),
            pltpu.VMEM((nt, tokens, chunk), bf16),
            pltpu.VMEM((nt, tokens, chunk), bf16),
            pltpu.VMEM((outward, slots // 2, tile), bf16),
            dma((3, nt)),
            dma((1,)),
            dma((nt, pieces, 2)),
            dma((nt, pieces, 2)),
            dma((nt, pieces, 2)),
            dma((nt, pieces, 2)),
            dma((nt,)),
            dma((nt,)),
            dma((nt,)),
            dma((nt,)),
            dma((inward,)),
            dma((outward,)),
            dma((outward,)),
        ],
        compiler_params=pltpu.CompilerParams(
            collective_id=0, has_side_effects=True, vmem_limit_bytes=67043328
        ),
    )(
        grad_out,
        expert_ids.T,
        gate_probs.T,
        live.reshape(1, tokens),
        w_gate,
        w_up,
        w_down,
        saved,
    )


def solution(mesh):
    placed = (
        P("expert", "tensor"),
        P("expert", None),
        P("expert", None),
        P("expert"),
        P("expert", "tensor", None),
        P("expert", "tensor", None),
        P("expert", "tensor", None),
        P("expert", None, "tensor", None),
    )
    return jax.shard_map(
        shards, mesh=mesh, in_specs=placed, out_specs=P("expert", "tensor"), check_vma=False
    )
```

```python
import functools

import jax
import jax.numpy as jnp
from jax import lax
from jax.experimental import pallas as pl
from jax.experimental.pallas import tpu as pltpu
from jax.sharding import PartitionSpec as P

MESH = pl.DeviceIdType.MESH
NT = (((1,), (1,)), ((), ()))
NN = (((1,), (0,)), ((), ()))


def dot(a, b, dims):
    return lax.dot_general(a, b, dims, preferred_element_type=jnp.float32)


def mate(me, step, size, sign):
    if size & (size - 1):
        return lax.rem(me + (sign * step) % size, size)
    out, bit = 0, 1
    while bit < size:
        mine = lax.rem(lax.div(me, bit), 2)
        out = out + (1 - mine if step & bit else mine) * bit
        bit *= 2
    return out


INWARD = ((1, 2), (2, 1))
OUTWARD = ((1, 2), (2, 1))


def shortcuts(nt, pieces, shares):
    across = [0] * nt
    for s, quarters in shares:
        if s < nt:
            across[s] = pieces * quarters // 4
    return across


def kernel(
    ne, nt, cap, raw0, ids, gates, live, w_gate, w_up, w_down, saved, out,
    wd, wg, wu, sv, svt, dh, sel, gs, back, outgoing, recv, orecv, raw, part, zrecv, zterm,
    w_sem, sv_sem, in_send, in_recv, out_send, out_recv, z_send, z_recv, p_send, p_recv,
    b_send, t_send, t_recv,
):
    me = lax.axis_index("expert")
    mz = lax.axis_index("tensor")
    tokens, chunk = raw0.shape
    slots = ne * cap
    hidden = saved.shape[2]
    tops = ids.shape[0]
    steps = range(nt)
    owner = [mate(mz, s, nt, 1) for s in steps]
    zpeer = [mate(mz, s, nt, -1) for s in steps]
    order = sorted(range(1, ne), key=lambda j: (-(j // 2) if j > 1 else 1, j))
    epeer = [mate(me, j, ne, 1) for j in order]

    barrier = pltpu.get_barrier_semaphore()
    for peer in epeer:
        pl.semaphore_signal(barrier, inc=1, device_id=(peer, mz), device_id_type=MESH)
    for s in range(1, nt):
        pl.semaphore_signal(barrier, inc=1, device_id=(me, zpeer[s]), device_id_type=MESH)

    def weight_copy(i, s):
        src = (w_down, w_gate, w_up)[i]
        dst = (wd, wg, wu)[i]
        columns = pl.ds(pl.multiple_of(owner[s] * chunk, chunk), chunk)
        return pltpu.make_async_copy(src.at[0, :, columns], dst.at[s], w_sem.at[i, s])

    saved_copy = pltpu.make_async_copy(saved.at[0], sv, sv_sem.at[0])

    tile = min(256, chunk)
    pieces = chunk // tile
    ahead = shortcuts(nt, pieces, INWARD)
    astern = shortcuts(nt, pieces, OUTWARD)
    halves = range(2)
    part_cap, part_slots = cap // 2, slots // 2

    def crossings(across):
        return [(s, j, h) for h in halves for s in steps for j in range(across[s])]

    def span(h):
        return pl.ds(h * part_slots, part_slots)

    def piece(j):
        return pl.ds(pl.multiple_of(j * tile, tile), tile)

    def build(src, s, j, h):
        picked = dot(sel[span(h), :], src[:, piece(j)], NN)
        outgoing[s, span(h), piece(j)] = (gs[span(h), :1] * picked).astype(jnp.bfloat16)

    def rows(h, e):
        return pl.ds(pl.multiple_of(h * part_slots + e * part_cap, part_cap), part_cap)

    def exchange(s, j, h, dst, send, receive):
        for peer in epeer:
            pltpu.make_async_remote_copy(
                src_ref=outgoing.at[s, rows(h, peer), piece(j)],
                dst_ref=dst.at[s, rows(h, me), piece(j)],
                send_sem=send.at[s, j, h],
                recv_sem=receive.at[s, j, h],
                device_id=(peer, mz),
                device_id_type=MESH,
            ).start()
        pltpu.make_async_copy(
            outgoing.at[s, rows(h, me), piece(j)],
            dst.at[s, rows(h, me), piece(j)],
            receive.at[s, j, h],
        ).start()

    def wait_all(ref, sem):
        pltpu.make_async_copy(ref, ref, sem).wait()

    def z_copy(src, dst, send, receive, peer):
        return pltpu.make_async_remote_copy(
            src_ref=src,
            dst_ref=dst,
            send_sem=send,
            recv_sem=receive,
            device_id=(me, peer),
            device_id_type=MESH,
        )

    def beyond(s, across):
        return pl.ds(across[s] * tile, chunk - across[s] * tile)

    pl.semaphore_wait(barrier, ne - 1 + nt - 1)
    z_copies = {
        s: z_copy(
            raw0.at[:, beyond(s, ahead)],
            raw.at[s, :, beyond(s, ahead)],
            z_send.at[s],
            z_recv.at[s],
            zpeer[s],
        )
        for s in range(1, nt)
    }
    for copy in z_copies.values():
        copy.start()

    experts = lax.broadcasted_iota(jnp.int32, (ne, tokens), 0)
    alive = live[...] != 0
    chosen = jnp.zeros((ne, tokens), jnp.float32)
    weight = jnp.zeros((ne, tokens), jnp.float32)
    for k in range(tops):
        match = (ids[k : k + 1, :] == experts) & alive
        chosen = chosen + jnp.where(match, 1.0, 0.0)
        weight = weight + jnp.where(match, gates[k : k + 1, :], 0.0)
    row = lax.broadcasted_iota(jnp.int32, (tokens, tokens), 0)
    col = lax.broadcasted_iota(jnp.int32, (tokens, tokens), 1)
    before = jnp.where(row < col, 1.0, 0.0).astype(jnp.bfloat16)
    position = dot(chosen.astype(jnp.bfloat16), before, NN)
    position = jnp.where((chosen > 0.0) & (position < cap), position, -1.0)
    slot = lax.broadcasted_iota(jnp.int32, (cap, tokens), 0).astype(jnp.float32)
    for e in range(ne):
        hit = slot == position[e : e + 1, :]
        gate = jnp.sum(jnp.where(hit, weight[e : e + 1, :], 0.0), axis=1, keepdims=True)
        gate = jnp.broadcast_to(gate, (cap, gs.shape[1]))
        hit = jnp.where(hit, 1.0, 0.0)
        for h in halves:
            some = slice(h * part_cap, (h + 1) * part_cap)
            sel[rows(h, e), :] = hit[some].astype(jnp.bfloat16)
            gs[rows(h, e), :] = gate[some]

    def give(src, s, which):
        @pl.loop(ahead[s], pieces)
        def _(j):
            for h in which:
                build(src, s, j, h)
                exchange(s, j, h, recv, in_send, in_recv)

    give(raw0, 0, halves)

    saved_copy.start()
    for s in steps:
        weight_copy(0, s).start()
    for s in reversed(steps):
        weight_copy(1, s).start()
        weight_copy(2, s).start()

    shared = {
        (s, j, h): z_copy(
            recv.at[0, span(h), piece(j)],
            recv.at[s, span(h), piece(j)],
            b_send.at[k],
            in_recv.at[s, j, h],
            zpeer[s],
        )
        for k, (s, j, h) in enumerate(crossings(ahead))
    }

    def landed(dst, s, j, h, receive):
        wait_all(dst.at[s, span(h), piece(j)], receive.at[s, j, h])

    early = max(1, nt // 2)
    for s in range(1, nt):
        z_copies[s].wait_recv()
        give(raw.at[s], s, halves if s < early else [0])
        if s == 1:
            for h in halves:
                for j in range(max(ahead)):
                    landed(recv, 0, j, h, in_recv)
            for copy in shared.values():
                copy.start()
    for s in range(early, nt):
        give(raw.at[s], s, [1])

    row = lax.broadcasted_iota(jnp.int32, (tokens, tokens), 0)
    col = lax.broadcasted_iota(jnp.int32, (tokens, tokens), 1)
    eye = jnp.where(row == col, 1.0, 0.0).astype(jnp.bfloat16)
    back[...] = dot(eye, sel[...], NT).astype(jnp.bfloat16)
    block = max(cap, min(128, slots))
    saved_copy.wait()

    @pl.loop(0, slots // block)
    def _(b):
        at = pl.ds(pl.multiple_of(b * block, block), block)
        r = lax.broadcasted_iota(jnp.int32, (block, block), 0)
        c = lax.broadcasted_iota(jnp.int32, (block, block), 1)
        one = jnp.where(r == c, 1.0, 0.0).astype(jnp.bfloat16)
        for i in range(2):
            turned = dot(one, sv[i, :, at], NT).astype(jnp.bfloat16)
            for g in range(block // cap):
                for h in halves:
                    some = slice(g * cap + h * part_cap, g * cap + (h + 1) * part_cap)
                    svt[i, rows(h, b * (block // cap) + g), :] = turned[some]

    def contract(s, h):
        for j in range(pieces):
            if s > 0 or nt == 1 or j >= max(ahead):
                landed(recv, s, j, h, in_recv)
        part_sum = dot(recv[s, span(h), :], wd[s], NT)
        dh[span(h), :] = part_sum if s == 0 else dh[span(h), :] + part_sum

    few = 16

    def activate(h):
        @pl.loop(h * part_slots // few, (h + 1) * part_slots // few)
        def _(b):
            at = pl.ds(pl.multiple_of(b * few, few), few)
            grad = dh[at, :]
            a = svt[0, at, :].astype(jnp.float32)
            u = svt[1, at, :].astype(jnp.float32)
            sig = jax.nn.sigmoid(a)
            svt[1, at, :] = (grad * a * sig).astype(jnp.bfloat16)
            svt[0, at, :] = (grad * u * sig * (1.0 + a * (1.0 - sig))).astype(jnp.bfloat16)

    def combine(s, j):
        return dot(back[...], orecv[s, :, piece(j)], NN)

    p_copies = {
        s: z_copy(
            part.at[s, :, beyond(s, astern)],
            zrecv.at[s, :, beyond(s, astern)],
            p_send.at[s],
            p_recv.at[s],
            owner[s],
        )
        for s in range(1, nt)
    }
    t_copies = {
        (s, j, h): z_copy(
            outgoing.at[s, span(h), piece(j)], zterm.at[k], t_send.at[k], t_recv.at[k], owner[s]
        )
        for k, (s, j, h) in enumerate(crossings(astern))
    }
    others = outgoing.at[0, pl.ds(0, (ne - 1) * part_cap), pl.ds(0, tile)]

    def term(s, j, h):
        total = dot(svt[0, span(h), :], wg[s, :, piece(j)], NN)
        return total + dot(svt[1, span(h), :], wu[s, :, piece(j)], NN)

    def vacant(s, j, h):
        wait_all(others, in_send.at[s, j, h])

    def hand(s, h, low, high):
        for first, end in ((low, min(high, ahead[s])), (max(low, ahead[s]), high)):
            if first < end:

                @pl.loop(first, end)
                def _(j):
                    if first >= ahead[s]:
                        vacant(s, j, h)
                    outgoing[s, span(h), piece(j)] = term(s, j, h).astype(jnp.bfloat16)
                    exchange(s, j, h, orecv, out_send, out_recv)

    def hand_across(s, h):
        for j in range(astern[s]):
            if j >= ahead[s]:
                vacant(s, j, h)
            outgoing[s, span(h), piece(j)] = term(s, j, h).astype(jnp.bfloat16)
            t_copies[s, j, h].start()

    last = nt - 1

    def send_back_own(h):
        for j in reversed(range(max(astern))):
            total = term(0, j, h)
            for k, (s, q, half) in enumerate(crossings(astern)):
                if q == j and half == h:
                    t_copies[s, q, h].wait_recv()
                    total = total + zterm[k].astype(jnp.float32)
            vacant(0, j, h)
            outgoing[0, span(h), piece(j)] = total.astype(jnp.bfloat16)
            exchange(0, j, h, orecv, out_send, out_recv)

    for s in steps:
        weight_copy(0, s).wait()
        contract(s, 0)
        if s == 0:
            contract(s, 1)
    activate(0)
    for s in steps:
        weight_copy(1, s).wait()
        weight_copy(2, s).wait()
    far = list(reversed(range(early, nt)))
    near = list(reversed(range(1, early)))
    for i, s in enumerate(far):
        hand(s, 0, astern[s], pieces)
        if i == 0:
            for q in range(1, nt):
                hand_across(q, 0)
    for s in range(1, nt):
        contract(s, 1)
    activate(1)
    for s in far:
        hand(s, 1, astern[s], pieces)
    for q in range(1, nt):
        hand_across(q, 1)
    for s in near:
        for h in halves:
            hand(s, h, astern[s], pieces)
    for h in halves:
        hand(0, h, max(astern), pieces)

    def finish(s):
        @pl.loop(astern[s], pieces)
        def _(j):
            for h in halves:
                landed(orecv, s, j, h, out_recv)
            part[s, :, piece(j)] = combine(s, j).astype(jnp.bfloat16)

        p_copies[s].start()

    for s in far:
        finish(s)
    for h in halves:
        send_back_own(h)

    for s in near:
        finish(s)
    for s in range(1, nt):
        p_copies[s].wait_recv()
    for j in [*range(max(astern), pieces), *reversed(range(max(astern)))]:
        for h in halves:
            landed(orecv, 0, j, h, out_recv)
        total = combine(0, j)
        for q in range(1, nt):
            if j >= astern[q]:
                total = total + zrecv[q, :, piece(j)].astype(jnp.float32)
        out[:, piece(j)] = total.astype(jnp.bfloat16)

    for s in steps:
        for j in range(pieces):
            for h in halves:
                if j >= astern[s]:
                    wait_all(others, out_send.at[s, j, h])
    for s in range(1, nt):
        z_copies[s].wait_send()
        p_copies[s].wait_send()
    for copy in [*shared.values(), *t_copies.values()]:
        copy.wait_send()


def shards(grad_out, expert_ids, gate_probs, live, w_gate, w_up, w_down, saved):
    ne = lax.axis_size("expert")
    nt = lax.axis_size("tensor")
    tokens, chunk = grad_out.shape
    cap = tokens * expert_ids.shape[1] // ne
    slots = ne * cap
    hidden = saved.shape[2]
    tile = min(256, chunk)
    pieces = chunk // tile
    inward = max(1, 2 * sum(shortcuts(nt, pieces, INWARD)))
    outward = max(1, 2 * sum(shortcuts(nt, pieces, OUTWARD)))
    bf16, f32 = jnp.bfloat16, jnp.float32
    vmem = pl.BlockSpec(memory_space=pltpu.VMEM)
    anywhere = pl.BlockSpec(memory_space=pl.ANY)
    dma = pltpu.SemaphoreType.DMA
    return pl.pallas_call(
        functools.partial(kernel, ne, nt, cap),
        out_shape=jax.ShapeDtypeStruct((tokens, chunk), bf16),
        in_specs=[vmem] * 4 + [anywhere] * 4,
        out_specs=vmem,
        scratch_shapes=[
            pltpu.VMEM((nt, hidden, chunk), bf16),
            pltpu.VMEM((nt, hidden, chunk), bf16),
            pltpu.VMEM((nt, hidden, chunk), bf16),
            pltpu.VMEM((2, hidden, slots), bf16),
            pltpu.VMEM((2, slots, hidden), bf16),
            pltpu.VMEM((slots, hidden), f32),
            pltpu.VMEM((slots, tokens), bf16),
            pltpu.VMEM((slots, 128), f32),
            pltpu.VMEM((tokens, slots), bf16),
            pltpu.VMEM((nt, slots, chunk), bf16),
            pltpu.VMEM((nt, slots, chunk), bf16),
            pltpu.VMEM((nt, slots, chunk), bf16),
            pltpu.VMEM((nt, tokens, chunk), bf16),
            pltpu.VMEM((nt, tokens, chunk), bf16),
            pltpu.VMEM((nt, tokens, chunk), bf16),
            pltpu.VMEM((outward, slots // 2, tile), bf16),
            dma((3, nt)),
            dma((1,)),
            dma((nt, pieces, 2)),
            dma((nt, pieces, 2)),
            dma((nt, pieces, 2)),
            dma((nt, pieces, 2)),
            dma((nt,)),
            dma((nt,)),
            dma((nt,)),
            dma((nt,)),
            dma((inward,)),
            dma((outward,)),
            dma((outward,)),
        ],
        compiler_params=pltpu.CompilerParams(
            collective_id=0, has_side_effects=True, vmem_limit_bytes=67043328
        ),
    )(
        grad_out,
        expert_ids.T,
        gate_probs.T,
        live.reshape(1, tokens),
        w_gate,
        w_up,
        w_down,
        saved,
    )


def solution(mesh):
    placed = (
        P("expert", "tensor"),
        P("expert", None),
        P("expert", None),
        P("expert"),
        P("expert", "tensor", None),
        P("expert", "tensor", None),
        P("expert", "tensor", None),
        P("expert", None, "tensor", None),
    )
    return jax.shard_map(
        shards, mesh=mesh, in_specs=placed, out_specs=P("expert", "tensor"), check_vma=False
    )
```
